256 devices in a mesh: view: 4 (over y_hi, core), row: 8 (over z), col: 8 (over y_lo, x).
Axes of the slice: x: 4, y: 4 (y_hi: 2, y_lo: 2; y = y_hi * 2 + y_lo), z: 8, core: 2. Of those that a mesh axis runs over, the one named last changes fastest.
Arguments:
- view_maps: bfloat16 [16, 32, 128, 768], P('view', 'row', 'col'), may hold values from -6 to 6
- gain_spatial: float32 [768], replicated, may hold values from 0.1 to 1.9
- spatial_query: bfloat16 [768, 768], replicated, may hold values from -8 to 8
- spatial_key: bfloat16 [768, 768], replicated, may hold values from -8 to 8
- spatial_value: bfloat16 [768, 768], replicated, may hold values from -0.21875 to 0.21875
- spatial_output: bfloat16 [768, 768], replicated, may hold values from -0.21875 to 0.21875
- gain_temporal: float32 [768], replicated, may hold values from 0.1 to 1.9
- temporal_query: bfloat16 [768, 768], replicated, may hold values from -8 to 8
- temporal_key: bfloat16 [768, 768], replicated, may hold values from -8 to 8
- temporal_value: bfloat16 [768, 768], replicated, may hold values from -0.21875 to 0.21875
- temporal_output: bfloat16 [768, 768], replicated, may hold values from -0.21875 to 0.21875
Outputs:
- refined: bfloat16 [16, 32, 128, 768], P('view', 'row', 'col')
The draws below stay inside these ranges and needn't reach their ends.
All inputs are finite; a program needn't handle non-finite values.
Results may differ from the reference program's by a relative error of at most 0.012.
Values may be sent and summed in bfloat16 or wider, within the bound.
No kernel may reach another device: no remote copies, remote signals or barrier semaphores. Data moves between devices by JAX's collectives and lax.ppermute only.
A program may use at most 64 MiB of HBM per device.

```python
import jax
import jax.numpy as jnp
from jax import lax

D = 768
HEADS = 12
HEAD_DIM = 64
RADIUS = 3
VIEWS = 16
MAP_H = 32
MAP_W = 128


def paired_weights(key, which):
    base = jax.random.fold_in(key, 100 + which)
    first = jax.random.normal(jax.random.fold_in(base, 1), (D, D), jnp.float32) * D ** (-0.5)
    second = jax.random.normal(jax.random.fold_in(base, 2), (D, D), jnp.float32) * D ** (-0.5)
    first = jnp.clip(first, -8.0, 8.0)
    second = jnp.clip(second, -8.0, 8.0)
    return (first.astype(jnp.bfloat16), second.astype(jnp.bfloat16))


def draw_spatial_query(key, part):
    return paired_weights(key, 0)[0]


def draw_spatial_key(key, part):
    return paired_weights(key, 0)[1]


def draw_temporal_query(key, part):
    return paired_weights(key, 1)[0]


def draw_temporal_key(key, part):
    return paired_weights(key, 1)[1]


def block_levels(own_key, extent, cuts, least, largest):
    gain, own = 1.0, jax.random.fold_in(own_key, 6)
    for dim, blocks in cuts:
        heights = jnp.exp(jax.random.uniform(jax.random.fold_in(own, dim), (blocks,), jnp.float32, least / len(cuts), largest / len(cuts)))
        gain = gain * jnp.repeat(heights, extent[dim] // blocks).reshape([-1 if axis == dim else 1 for axis in range(len(extent))])
    return gain


def noise(stream_key, extent, scale, bound, cuts=(), held_as=jnp.bfloat16):
    level = block_levels(stream_key, extent, cuts, -0.22, 0.18) if cuts else 1.0
    values = jax.random.normal(stream_key, extent, jnp.float32) * scale * level
    return jnp.minimum(jnp.maximum(values, -bound), bound).astype(held_as)


def setup_inputs(seed: int = 0) -> dict:
    splits = jax.random.split(jax.random.key(seed), 12)
    view_maps = noise(splits[0], (VIEWS, MAP_H, MAP_W, D), 1.0, 6.0, ((0, 4), (1, 8), (2, 8)))
    gain_spatial = jnp.clip(1.0 + 0.18 * jax.random.normal(splits[1], (D,), jnp.float32), 0.1, 1.9)
    spatial_query = draw_spatial_query(jax.random.fold_in(splits[11], 71), 0)
    spatial_key = draw_spatial_key(jax.random.fold_in(splits[11], 71), 0)
    spatial_value = noise(splits[4], (D, D), D ** -0.5, 0.21875)
    spatial_output = noise(splits[5], (D, D), D ** -0.5, 0.21875)
    gain_temporal = jnp.clip(1.0 + 0.18 * jax.random.normal(splits[6], (D,), jnp.float32), 0.1, 1.9)
    temporal_query = draw_temporal_query(jax.random.fold_in(splits[11], 71), 0)
    temporal_key = draw_temporal_key(jax.random.fold_in(splits[11], 71), 0)
    temporal_value = noise(splits[9], (D, D), D ** -0.5, 0.21875)
    temporal_output = noise(splits[10], (D, D), D ** -0.5, 0.21875)
    return dict(view_maps=view_maps, gain_spatial=gain_spatial, spatial_query=spatial_query, spatial_key=spatial_key, spatial_value=spatial_value, spatial_output=spatial_output, gain_temporal=gain_temporal, temporal_query=temporal_query, temporal_key=temporal_key, temporal_value=temporal_value, temporal_output=temporal_output)


epsilon = 1e-06
very_negative = -1e+30

def rms_norm(tokens, gain_vector):
    values = tokens.astype(jnp.float32)
    scaled = values * lax.rsqrt(lax.optimization_barrier(jnp.mean(values * values, axis=-1, keepdims=True)) + epsilon)
    return (scaled * gain_vector).astype(jnp.bfloat16)

def project(tokens, weight_matrix):
    flat = tokens.reshape(-1, tokens.shape[-1])
    result = jnp.dot(flat, weight_matrix, preferred_element_type=jnp.float32)
    return result.reshape(tokens.shape[:-1] + (weight_matrix.shape[1],))

def neighbour(queries, keys_wide, values_wide, row_places, col_places, total_rows, total_cols):
    height, width = (queries.shape[1], queries.shape[2])
    head_shape = queries.shape[:-1] + (HEADS, HEAD_DIM)
    query_float = queries.astype(jnp.float32).reshape(head_shape)
    factor = HEAD_DIM ** (-0.5)
    score_list = []
    valid_list = []
    span = 2 * RADIUS + 1
    for offset_row in range(span):
        for offset_col in range(span):
            shifted = keys_wide[:, offset_row:offset_row + height, offset_col:offset_col + width, :]
            shifted = shifted.astype(jnp.float32).reshape(head_shape)
            score_list.append(lax.optimization_barrier(jnp.sum(query_float * shifted, axis=-1)) * factor)
            rows_there = row_places + offset_row - RADIUS
            cols_there = col_places + offset_col - RADIUS
            rows_fine = (rows_there >= 0) & (rows_there < total_rows)
            cols_fine = (cols_there >= 0) & (cols_there < total_cols)
            valid_list.append(rows_fine[:, None] & cols_fine[None, :])
    scores = jnp.stack(score_list, 0)
    valid = jnp.stack(valid_list, 0)[:, None, :, :, None]
    scores = jnp.where(valid, scores, very_negative)
    highest = lax.optimization_barrier(jnp.max(scores, axis=0))
    weights = jnp.exp(scores - highest)
    weights = weights / lax.optimization_barrier(jnp.sum(weights, axis=0))
    total = jnp.zeros(head_shape, jnp.float32)
    index = 0
    for offset_row in range(span):
        for offset_col in range(span):
            shifted = values_wide[:, offset_row:offset_row + height, offset_col:offset_col + width, :]
            shifted = shifted.astype(jnp.float32).reshape(head_shape)
            total = total + weights[index][..., None] * shifted
            index = index + 1
    return total.reshape(queries.shape).astype(jnp.bfloat16)

def reference(view_maps, gain_spatial, spatial_query, spatial_key, spatial_value, spatial_output, gain_temporal, temporal_query, temporal_key, temporal_value, temporal_output):
    normed = rms_norm(view_maps, gain_spatial)
    queries = project(normed, spatial_query).astype(jnp.bfloat16)
    keys = project(normed, spatial_key).astype(jnp.bfloat16)
    values = project(normed, spatial_value).astype(jnp.bfloat16)
    padding = ((0, 0), (RADIUS, RADIUS), (RADIUS, RADIUS), (0, 0))
    keys_wide = jnp.pad(keys, padding)
    values_wide = jnp.pad(values, padding)
    row_places = jnp.arange(MAP_H, dtype=jnp.int32)
    col_places = jnp.arange(MAP_W, dtype=jnp.int32)

    def per_view(items):
        return neighbour(items[0][None], items[1][None], items[2][None], row_places, col_places, MAP_H, MAP_W)[0]
    attended = lax.map(per_view, (queries, keys_wide, values_wide))
    middle = (view_maps.astype(jnp.float32) + project(attended, spatial_output)).astype(jnp.bfloat16)
    normed_time = rms_norm(middle, gain_temporal)
    query_time = project(normed_time, temporal_query).astype(jnp.bfloat16)
    key_time = project(normed_time, temporal_key).astype(jnp.bfloat16)
    value_time = project(normed_time, temporal_value).astype(jnp.bfloat16)
    factor = HEAD_DIM ** (-0.5)

    def per_row(items):
        shape_heads = items[0].shape[:-1] + (HEADS, HEAD_DIM)
        query_float = items[0].astype(jnp.float32).reshape(shape_heads)
        key_float = items[1].astype(jnp.float32).reshape(shape_heads)
        value_float = items[2].astype(jnp.float32).reshape(shape_heads)
        scores = jnp.einsum('qthe,kthe->qkth', query_float, key_float) * factor
        highest = lax.optimization_barrier(jnp.max(scores, axis=1, keepdims=True))
        weights = jnp.exp(scores - highest)
        weights = weights / lax.optimization_barrier(jnp.sum(weights, axis=1, keepdims=True))
        mixed = jnp.einsum('qkth,kthe->qthe', weights, value_float)
        return mixed.reshape(items[0].shape).astype(jnp.bfloat16)
    moved = lax.map(per_row, (jnp.swapaxes(query_time, 0, 1), jnp.swapaxes(key_time, 0, 1), jnp.swapaxes(value_time, 0, 1)))
    attended_time = jnp.swapaxes(moved, 0, 1)
    refined = (middle.astype(jnp.float32) + project(attended_time, temporal_output)).astype(jnp.bfloat16)
    return refined
```

```python
import functools

import jax
import jax.numpy as jnp
from jax import lax
from jax.experimental import pallas as pl
from jax.experimental.pallas import tpu as pltpu
from jax.sharding import PartitionSpec as P

HEADS = 12
HEAD_DIM = 64
RADIUS = 3
D = 768
GROUP = 4
LANES = GROUP * HEAD_DIM
GROUPS = HEADS // GROUP
ROWS = 4
COLS = 16
TOKENS = ROWS * COLS
SLAB = RADIUS * COLS
SIDE = 32
KEYS = TOKENS + 2 * SLAB + 2 * SIDE
VIEWS = 4
ALL_VIEWS = 16
MAP_H = 32
MAP_W = 128

epsilon = 1e-06
very_negative = -1e30
BF = jnp.bfloat16
F32 = jnp.float32
MIB = 1 << 20


def call(body, outs, flops, nbytes, scratch=(), smem_first=False, n_in=0, limit=20, name=None):
    vmem = pl.BlockSpec(memory_space=pltpu.VMEM)
    in_specs = [vmem] * n_in
    if smem_first:
        in_specs[0] = pl.BlockSpec(memory_space=pltpu.SMEM)
    return pl.pallas_call(
        body,
        out_shape=tuple(jax.ShapeDtypeStruct(s, BF) for s in outs),
        in_specs=in_specs,
        out_specs=tuple(vmem for _ in outs),
        scratch_shapes=list(scratch),
        compiler_params=pltpu.CompilerParams(vmem_limit_bytes=limit * MIB),
        cost_estimate=pl.CostEstimate(flops=flops, bytes_accessed=nbytes, transcendentals=0),
        name=name,
    )


def normed(tokens, gain):
    values = tokens.astype(F32)
    mean = jnp.mean(values * values, axis=-1, keepdims=True)
    return (values * lax.rsqrt(mean + epsilon) * gain).astype(BF)


def dot(a, b):
    return jnp.dot(a, b, preferred_element_type=F32)


def own_body(x, gain, wq, wk, wv, q, k, v):
    n = normed(x[...], gain[...])
    q[...] = dot(n, wq[...]).astype(BF)
    k[...] = dot(n, wk[...]).astype(BF)
    v[...] = dot(n, wv[...]).astype(BF)


def sides_body(x, up, down, to_left, to_right):
    i = lax.broadcasted_iota(jnp.int32, (2 * SIDE, TOKENS + 2 * SLAB), 0)
    j = lax.broadcasted_iota(jnp.int32, (2 * SIDE, TOKENS + 2 * SLAB), 1)
    place = RADIUS * (j >> 4) + (j & 15)
    first = ((j & 15) < RADIUS) & (i == place)
    last = ((j & 15) >= COLS - RADIUS) & (i - SIDE == place - (COLS - RADIUS))
    pick = jnp.where(first | last, 1.0, 0.0).astype(BF)
    for view in range(VIEWS):
        wide = jnp.concatenate([up[view], x[view], down[view]], axis=0)
        taken = dot(pick, wide).astype(BF)
        to_left[view] = taken[:SIDE]
        to_right[view] = taken[SIDE:]


def slabs_body(up, down, gain, wk, wv, ku, vu, kd, vd):
    for source, k, v in ((up, ku, vu), (down, kd, vd)):
        n = normed(source[...], gain[...])
        k[...] = dot(n, wk[...]).astype(BF)
        v[...] = dot(n, wv[...]).astype(BF)


def attend(q, keys, values, allowed, spread):
    stacked = jnp.concatenate([q] * GROUP, axis=0)
    stacked = jnp.where(spread, stacked, jnp.zeros_like(stacked))
    scores = lax.dot_general(stacked, keys, (((1,), (1,)), ((), ())), preferred_element_type=F32)
    scores = jnp.where(allowed, scores, very_negative)
    highest = jnp.max(scores, axis=-1, keepdims=True)
    weights = jnp.exp(scores - highest)
    total = jnp.sum(weights, axis=-1, keepdims=True)
    mixed = dot(weights.astype(BF), values) / total
    mixed = jnp.where(spread, mixed, 0.0)
    count = q.shape[0]
    result = mixed[:count]
    for head in range(1, GROUP):
        result = result + mixed[head * count:(head + 1) * count]
    return result.astype(BF)


def spread_mask(count):
    shape = (GROUP * count, LANES)
    row = lax.broadcasted_iota(jnp.int32, shape, 0)
    lane = lax.broadcasted_iota(jnp.int32, shape, 1)
    return (row // count) == (lane // HEAD_DIM)


def window_mask(first_row, first_col):
    shape = (GROUP * TOKENS, KEYS)
    i = lax.broadcasted_iota(jnp.int32, shape, 0) & (TOKENS - 1)
    query_row, query_col = i >> 4, i & 15
    j = lax.broadcasted_iota(jnp.int32, shape, 1)
    up, down, left, right = TOKENS, TOKENS + SLAB, TOKENS + 2 * SLAB, TOKENS + 2 * SLAB + SIDE
    row = jnp.where(j < up, j >> 4, jnp.where(j < down, ((j - up) >> 4) - RADIUS, ((j - down) >> 4) + ROWS))
    col = j & 15
    t = (j - left) & (SIDE - 1)
    t_row = (t * 43) >> 7
    t_col = t - 3 * t_row
    side = j >= left
    row = jnp.where(side, t_row - RADIUS, row)
    col = jnp.where(side, jnp.where(j >= right, t_col + COLS, t_col - RADIUS), col)
    real = jnp.logical_not(side) | (t < RADIUS * (ROWS + 2 * RADIUS))
    near = (jnp.abs(row - query_row) <= RADIUS) & (jnp.abs(col - query_col) <= RADIUS)
    there_row, there_col = first_row + row, first_col + col
    inside = (there_row >= 0) & (there_row < MAP_H) & (there_col >= 0) & (there_col < MAP_W)
    return real & near & inside


def window_body(place, x, q, k, v, ku, vu, kd, vd, left, right, gain, wk, wv, wo, middle, side_k, side_v, out):
    sides = normed(jnp.concatenate([left[...], right[...]], axis=0), gain[...])
    side_k[...] = dot(sides, wk[...]).astype(BF)
    side_v[...] = dot(sides, wv[...]).astype(BF)
    allowed = window_mask(place[0], place[1])
    spread = spread_mask(TOKENS)
    half = VIEWS * SIDE
    for view in range(VIEWS):
        t = slice(view * TOKENS, (view + 1) * TOKENS)
        s = slice(view * SLAB, (view + 1) * SLAB)
        lo = slice(view * SIDE, (view + 1) * SIDE)
        hi = slice(half + view * SIDE, half + (view + 1) * SIDE)
        for group in range(GROUPS):
            f = slice(group * LANES, (group + 1) * LANES)
            keys = jnp.concatenate([k[t, f], ku[s, f], kd[s, f], side_k[lo, f], side_k[hi, f]], axis=0)
            values = jnp.concatenate([v[t, f], vu[s, f], vd[s, f], side_v[lo, f], side_v[hi, f]], axis=0)
            out[t, f] = attend(q[t, f] * 0.125, keys, values, allowed, spread)
    middle[...] = (x[...].astype(F32) + dot(out[...], wo[...])).astype(BF)


def near_body(m, partner, gain, wq, wk, wv, q, k, v, kp, vp):
    own_body(m, gain, wq, wk, wv, q, k, v)
    n = normed(partner[...], gain[...])
    kp[...] = dot(n, wk[...]).astype(BF)
    vp[...] = dot(n, wv[...]).astype(BF)


def views_body(m, q, k, v, kp, vp, far, far_partner, gain, wk, wv, wo, refined, kf, vf, out):
    n = normed(jnp.concatenate([far[...], far_partner[...]], axis=0), gain[...])
    kf[...] = dot(n, wk[...]).astype(BF)
    vf[...] = dot(n, wv[...]).astype(BF)
    spread = spread_mask(TOKENS)
    shape = (GROUP * TOKENS, ALL_VIEWS * COLS)
    i = lax.broadcasted_iota(jnp.int32, shape, 0)
    j = lax.broadcasted_iota(jnp.int32, shape, 1)
    allowed = (i & 15) == (j & 15)
    own = VIEWS * TOKENS

    def rows(ref, row, f, base=0):
        return [ref[base + w * TOKENS + row * COLS:base + w * TOKENS + (row + 1) * COLS, f] for w in range(VIEWS)]

    for row in range(ROWS):
        for group in range(GROUPS):
            f = slice(group * LANES, (group + 1) * LANES)
            queries = jnp.concatenate(rows(q, row, f), axis=0)
            keys = jnp.concatenate(rows(k, row, f) + rows(kp, row, f) + rows(kf, row, f) + rows(kf, row, f, own), axis=0)
            values = jnp.concatenate(rows(v, row, f) + rows(vp, row, f) + rows(vf, row, f) + rows(vf, row, f, own), axis=0)
            mixed = attend(queries * 0.125, keys, values, allowed, spread)
            for w in range(VIEWS):
                out[w * TOKENS + row * COLS:w * TOKENS + (row + 1) * COLS, f] = mixed[w * COLS:(w + 1) * COLS]
    refined[...] = (m[...].astype(F32) + dot(out[...], wo[...])).astype(BF)


def body(
    view_maps,
    gain_spatial,
    spatial_query,
    spatial_key,
    spatial_value,
    spatial_output,
    gain_temporal,
    temporal_query,
    temporal_key,
    temporal_value,
    temporal_output,
):
    own = VIEWS * TOKENS
    x = view_maps.reshape(own, D)
    gain_s = gain_spatial.reshape(1, D)
    gain_t = gain_temporal.reshape(1, D)
    place = jnp.stack([lax.axis_index("row") * ROWS, lax.axis_index("col") * COLS]).astype(jnp.int32)
    forward = [(i, i + 1) for i in range(7)]
    backward = [(i + 1, i) for i in range(7)]
    up = lax.ppermute(view_maps[:, ROWS - RADIUS:], "row", forward)
    down = lax.ppermute(view_maps[:, :RADIUS], "row", backward)
    q, k, v = call(own_body, [(own, D)] * 3, 2 * own * D * D * 3, 6 * MIB, n_in=5, name="own")(
        x, gain_s, spatial_query, spatial_key, spatial_value)
    up = up.reshape(VIEWS, SLAB, D)
    down = down.reshape(VIEWS, SLAB, D)
    to_left, to_right = call(sides_body, [(VIEWS, SIDE, D)] * 2, 10**8, 2 * MIB, n_in=3, name="sides")(
        x.reshape(VIEWS, TOKENS, D), up, down)
    left = lax.ppermute(to_right, "col", forward)
    right = lax.ppermute(to_left, "col", backward)
    slab = VIEWS * SLAB
    ku, vu, kd, vd = call(slabs_body, [(slab, D)] * 4, 2 * slab * D * D * 4, 6 * MIB, n_in=5, name="slabs")(
        up.reshape(slab, D), down.reshape(slab, D), gain_s, spatial_key, spatial_value)
    side = VIEWS * SIDE
    (middle,) = call(
        window_body, [(own, D)], 10**9, 8 * MIB, n_in=15, smem_first=True, name="window",
        scratch=[pltpu.VMEM((2 * side, D), BF), pltpu.VMEM((2 * side, D), BF), pltpu.VMEM((own, D), BF)],
    )(place, x, q, k, v, ku, vu, kd, vd, left.reshape(side, D), right.reshape(side, D), gain_s,
      spatial_key, spatial_value, spatial_output)
    far = lax.ppermute(middle, "view", [(i, i ^ 2) for i in range(4)])
    partner = lax.ppermute(middle, "view", [(i, i ^ 1) for i in range(4)])
    q, k, v, kp, vp = call(near_body, [(own, D)] * 5, 2 * own * D * D * 5, 8 * MIB, n_in=6, name="near")(
        middle, partner, gain_t, temporal_query, temporal_key, temporal_value)
    far_partner = lax.ppermute(far, "view", [(i, i ^ 1) for i in range(4)])
    (refined,) = call(
        views_body, [(own, D)], 10**9, 8 * MIB, n_in=12, name="views",
        scratch=[pltpu.VMEM((2 * own, D), BF), pltpu.VMEM((2 * own, D), BF), pltpu.VMEM((own, D), BF)],
    )(middle, q, k, v, kp, vp, far, far_partner, gain_t, temporal_key, temporal_value, temporal_output)
    return refined.reshape(view_maps.shape)


def solution(mesh):
    return jax.shard_map(
        body,
        mesh=mesh,
        in_specs=(P("view", "row", "col", None), P(), P(), P(), P(), P(), P(), P(), P(), P(), P()),
        out_specs=P("view", "row", "col", None),
        check_vma=False,
    )
```

```python
import functools

import jax
import jax.numpy as jnp
from jax import lax
from jax.experimental import pallas as pl
from jax.experimental.pallas import tpu as pltpu
from jax.sharding import PartitionSpec as P


HEADS = 12
HEAD_DIM = 64
RADIUS = 3
CHUNKS = 2
D = 768
GROUP = 4
LANES = GROUP * HEAD_DIM
GROUPS = HEADS // GROUP
ROWS = 4
COLS = 16
TOKENS = ROWS * COLS
SLAB = RADIUS * COLS
SIDE = 32
KEYS = TOKENS + 2 * SLAB + 2 * SIDE
VIEWS = 4
PART = VIEWS // CHUNKS
ALL_VIEWS = 16
MAP_H = 32
MAP_W = 128

epsilon = 1e-06
very_negative = -1e30
BF = jnp.bfloat16
F32 = jnp.float32
MIB = 1 << 20


def call(body, outs, flops, nbytes, scratch=(), n_in=0, limit=20):
    vmem = pl.BlockSpec(memory_space=pltpu.VMEM)
    return pl.pallas_call(
        body,
        out_shape=tuple(jax.ShapeDtypeStruct(s, BF) if isinstance(s, tuple) else s for s in outs),
        in_specs=[vmem] * n_in,
        out_specs=tuple(vmem for _ in outs),
        scratch_shapes=list(scratch),
        compiler_params=pltpu.CompilerParams(vmem_limit_bytes=limit * MIB),
        cost_estimate=pl.CostEstimate(flops=flops, bytes_accessed=nbytes, transcendentals=0),
    )


def normed(tokens, gain):
    values = tokens.astype(F32)
    mean = jnp.mean(values * values, axis=-1, keepdims=True)
    return (values * lax.rsqrt(mean + epsilon) * gain).astype(BF)


def dot(a, b):
    return jnp.dot(a, b, preferred_element_type=F32)


def own_body(x, gain, wq, wk, wv, q, k, v):
    n = normed(x[...], gain[...])
    q[...] = dot(n, wq[...]).astype(BF)
    k[...] = dot(n, wk[...]).astype(BF)
    v[...] = dot(n, wv[...]).astype(BF)


def sides_body(x, a, b, to_a, to_b):
    shape = (2 * SIDE, TOKENS + 2 * SLAB)
    i = lax.broadcasted_iota(jnp.int32, shape, 0)
    j = lax.broadcasted_iota(jnp.int32, shape, 1)
    odd = lax.axis_index("col") & 1
    base = jnp.where((i >= SIDE) == (odd == 1), COLS - RADIUS, 0)
    t = i & (SIDE - 1)
    col = (j & 15) - base
    chosen = (col >= 0) & (col < RADIUS) & (t == RADIUS * (j >> 4) + col)
    pick = jnp.where(chosen, 1.0, 0.0).astype(BF)
    for view in range(VIEWS):
        own = view * TOKENS
        wide = jnp.concatenate([a[view], x[own:own + TOKENS], b[view]], axis=0)
        taken = dot(pick, wide).astype(BF)
        to_a[view] = taken[:SIDE]
        to_b[view] = taken[SIDE:]


def slabs_body(a, b, gain, wk, wv, ka, va, kb, vb):
    for source, k, v in ((a, ka, va), (b, kb, vb)):
        n = normed(source[...], gain[...])
        k[...] = dot(n, wk[...]).astype(BF)
        v[...] = dot(n, wv[...]).astype(BF)


def compact(full, spread):
    full = jnp.where(spread, full, 0.0)
    count = full.shape[0] // GROUP
    result = full[:count]
    for head in range(1, GROUP):
        result = result + full[head * count:(head + 1) * count]
    return result


def partial_attend(q, keys, values, allowed, spread):
    stacked = jnp.concatenate([q] * GROUP, axis=0)
    stacked = jnp.where(spread, stacked, jnp.zeros_like(stacked))
    scores = lax.dot_general(stacked, keys, (((1,), (1,)), ((), ())), preferred_element_type=F32)
    scores = jnp.where(allowed, scores, very_negative)
    highest = jnp.max(scores, axis=-1, keepdims=True)
    weights = jnp.exp(scores - highest)
    total = jnp.sum(weights, axis=-1, keepdims=True)
    return dot(weights.astype(BF), values), highest, total


def attend(q, keys, values, allowed, spread):
    mixed, _, total = partial_attend(q, keys, values, allowed, spread)
    return compact(mixed / total, spread).astype(BF)


def spread_mask(count):
    shape = (GROUP * count, LANES)
    row = lax.broadcasted_iota(jnp.int32, shape, 0)
    lane = lax.broadcasted_iota(jnp.int32, shape, 1)
    return (row // count) == (lane // HEAD_DIM)


def window_mask(first_row, first_col):
    flat = (1, KEYS)
    j = lax.broadcasted_iota(jnp.int32, flat, 1)
    odd_row = ((first_row >> 2) & 1) == 1
    odd_col = ((first_col >> 4) & 1) == 1
    base_a = jnp.where(odd_row, -RADIUS, ROWS)
    base_b = jnp.where(odd_row, ROWS, -RADIUS)
    slab_a, slab_b, side_a, side_b = TOKENS, TOKENS + SLAB, TOKENS + 2 * SLAB, TOKENS + 2 * SLAB + SIDE
    row = jnp.where(j < slab_a, j >> 4, jnp.where(j < slab_b, ((j - slab_a) >> 4) + base_a, ((j - slab_b) >> 4) + base_b))
    t = (j - side_a) & (SIDE - 1)
    t_row = (t * 43) >> 7
    t_col = t - RADIUS * t_row
    wide_row = jnp.where(t_row < RADIUS, t_row + base_a, jnp.where(t_row < RADIUS + ROWS, t_row - RADIUS, t_row - RADIUS - ROWS + base_b))
    side = j >= side_a
    row = jnp.where(side, wide_row, row)
    at_right = (j >= side_b) == odd_col
    col = jnp.where(side, jnp.where(at_right, t_col + COLS, t_col - RADIUS), j & 15)
    real = jnp.logical_not(side) | (t < RADIUS * (ROWS + 2 * RADIUS))
    there_row, there_col = first_row + row, first_col + col
    inside = (there_row >= 0) & (there_row < MAP_H) & (there_col >= 0) & (there_col < MAP_W)
    row = jnp.where(real & inside, row, 1000)
    shape = (TOKENS, KEYS)
    i = lax.broadcasted_iota(jnp.int32, shape, 0)
    near = (jnp.abs(row - (i >> 4)) <= RADIUS) & (jnp.abs(col - (i & 15)) <= RADIUS)
    tall = jnp.concatenate([near.astype(jnp.int32)] * GROUP, axis=0)
    return tall > 0


def window_body(chunk, x, q, k, v, ka, va, kb, vb, side_a, side_b, gain, wk, wv, wo, middle, side_k, side_v, out):
    first = chunk * PART
    views = slice(first * SIDE, (first + PART) * SIDE)
    sides = normed(jnp.concatenate([side_a[views], side_b[views]], axis=0), gain[...])
    side_k[...] = dot(sides, wk[...]).astype(BF)
    side_v[...] = dot(sides, wv[...]).astype(BF)
    allowed = window_mask(lax.axis_index("row") * ROWS, lax.axis_index("col") * COLS)
    spread = spread_mask(TOKENS)
    half = PART * SIDE
    for view in range(PART):
        o = slice(view * TOKENS, (view + 1) * TOKENS)
        t = slice((first + view) * TOKENS, (first + view + 1) * TOKENS)
        s = slice((first + view) * SLAB, (first + view + 1) * SLAB)
        lo = slice(view * SIDE, (view + 1) * SIDE)
        hi = slice(half + view * SIDE, half + (view + 1) * SIDE)
        for group in range(GROUPS):
            f = slice(group * LANES, (group + 1) * LANES)
            keys = jnp.concatenate([k[t, f], ka[s, f], kb[s, f], side_k[lo, f], side_k[hi, f]], axis=0)
            values = jnp.concatenate([v[t, f], va[s, f], vb[s, f], side_v[lo, f], side_v[hi, f]], axis=0)
            out[o, f] = attend(q[t, f] * 0.125, keys, values, allowed, spread)
    middle[...] = (x[first * TOKENS:(first + PART) * TOKENS].astype(F32) + dot(out[...], wo[...])).astype(BF)


def same_place(count):
    shape = (GROUP * TOKENS, count)
    i = lax.broadcasted_iota(jnp.int32, shape, 0)
    j = lax.broadcasted_iota(jnp.int32, shape, 1)
    return (i & 15) == (j & 15)


def row_of(refs, row, f):
    return jnp.concatenate(
        [ref[w * TOKENS + row * COLS:w * TOKENS + (row + 1) * COLS, f] for ref in refs for w in range(ref.shape[0] // TOKENS)],
        axis=0,
    )


def near_body(*refs):
    middles, partners = refs[:CHUNKS], refs[CHUNKS:2 * CHUNKS]
    gain, wq, wk, wv, q, mixed, highest, total, k, v, kp, vp = refs[2 * CHUNKS:]
    n = normed(jnp.concatenate([r[...] for r in middles], axis=0), gain[...])
    q[...] = (dot(n, wq[...]).astype(BF) * 0.125).astype(BF)
    k[...] = dot(n, wk[...]).astype(BF)
    v[...] = dot(n, wv[...]).astype(BF)
    n = normed(jnp.concatenate([r[...] for r in partners], axis=0), gain[...])
    kp[...] = dot(n, wk[...]).astype(BF)
    vp[...] = dot(n, wv[...]).astype(BF)
    spread = spread_mask(TOKENS)
    allowed = same_place(ALL_VIEWS // 2 * COLS)
    for row in range(ROWS):
        t = slice(row * TOKENS, (row + 1) * TOKENS)
        for group in range(GROUPS):
            f = slice(group * LANES, (group + 1) * LANES)
            m, h, s = partial_attend(row_of([q], row, f), row_of([k, kp], row, f), row_of([v, vp], row, f), allowed, spread)
            mixed[t, f] = compact(m, spread)
            highest[t, f] = compact(h, spread)
            total[t, f] = compact(s, spread)


def far_body(far, gain, wk, wv, k, v):
    n = normed(far[...], gain[...])
    k[...] = dot(n, wk[...]).astype(BF)
    v[...] = dot(n, wv[...]).astype(BF)


def views_body(*refs):
    middles, (q, mixed, highest, total) = refs[:CHUNKS], refs[CHUNKS:CHUNKS + 4]
    refs = refs[CHUNKS + 4:]
    keys, values = list(refs[:2 * CHUNKS - 1]), list(refs[2 * CHUNKS - 1:4 * CHUNKS - 2])
    last, gain, wk, wv, wo, refined, kl, vl, out = refs[4 * CHUNKS - 2:]
    far_body(last, gain, wk, wv, kl, vl)
    keys.append(kl)
    values.append(vl)
    spread = spread_mask(TOKENS)
    allowed = same_place(ALL_VIEWS // 2 * COLS)
    for row in range(ROWS):
        t = slice(row * TOKENS, (row + 1) * TOKENS)
        for group in range(GROUPS):
            f = slice(group * LANES, (group + 1) * LANES)
            m, h, s = partial_attend(row_of([q], row, f), row_of(keys, row, f), row_of(values, row, f), allowed, spread)
            m, h, s = compact(m, spread), compact(h, spread), compact(s, spread)
            top = jnp.maximum(h, highest[t, f])
            late, early = jnp.exp(h - top), jnp.exp(highest[t, f] - top)
            full = (m * late + mixed[t, f] * early) / (s * late + total[t, f] * early)
            full = full.astype(BF)
            for w in range(VIEWS):
                out[w * TOKENS + row * COLS:w * TOKENS + (row + 1) * COLS, f] = full[w * COLS:(w + 1) * COLS]
    middle = jnp.concatenate([r[...] for r in middles], axis=0)
    refined[...] = (middle.astype(F32) + dot(out[...], wo[...])).astype(BF)


def swap(value, axis, first):
    count = lax.axis_size(axis)
    pairs = [(i, i + 1) for i in range(first, count - 1, 2)]
    return lax.ppermute(value, axis, pairs + [(j, i) for i, j in pairs])


def across(value, step):
    return lax.ppermute(value, "view", [(i, i ^ step) for i in range(4)])


def body(
    view_maps,
    gain_spatial,
    spatial_query,
    spatial_key,
    spatial_value,
    spatial_output,
    gain_temporal,
    temporal_query,
    temporal_key,
    temporal_value,
    temporal_output,
):
    own = VIEWS * TOKENS
    part = PART * TOKENS
    x = view_maps.reshape(own, D)
    gain_s = gain_spatial.reshape(1, D)
    gain_t = gain_temporal.reshape(1, D)
    odd = lax.axis_index("row") & 1
    a = swap(lax.dynamic_slice_in_dim(view_maps, 1 - odd, RADIUS, axis=1), "row", 0)
    b = swap(lax.dynamic_slice_in_dim(view_maps, odd, RADIUS, axis=1), "row", 1)
    q, k, v = call(own_body, [(own, D)] * 3, 2 * own * D * D * 3, 6 * MIB, n_in=5)(
        x, gain_s, spatial_query, spatial_key, spatial_value)
    slab, side = VIEWS * SLAB, VIEWS * SIDE
    to_a, to_b = call(sides_body, [(VIEWS, SIDE, D)] * 2, 10**8, 2 * MIB, n_in=3)(
        x, a.reshape(VIEWS, SLAB, D), b.reshape(VIEWS, SLAB, D))
    side_a = swap(to_a, "col", 0).reshape(side, D)
    side_b = swap(to_b, "col", 1).reshape(side, D)
    kv = call(slabs_body, [(slab, D)] * 4, 2 * slab * D * D * 4, 6 * MIB, n_in=5)(
        a.reshape(slab, D), b.reshape(slab, D), gain_s, spatial_key, spatial_value)
    middles, fars, partners = [], [], []
    for c in range(CHUNKS):
        (middle,) = call(
            functools.partial(window_body, c), [(part, D)], 10**9, 8 * MIB, n_in=14,
            scratch=[pltpu.VMEM((2 * PART * SIDE, D), BF), pltpu.VMEM((2 * PART * SIDE, D), BF), pltpu.VMEM((part, D), BF)],
        )(x, q, k, v, *kv, side_a, side_b, gain_s, spatial_key, spatial_value, spatial_output)
        middles.append(middle)
        fars.append(across(middle, 2))
        partners.append(across(middle, 1))
    big = jax.ShapeDtypeStruct((own, D), F32)
    rows = [pltpu.VMEM((own, D), BF)] * 4
    state = call(near_body, [(own, D), big, big, big], 4 * own * D * D * 5, 8 * MIB, n_in=2 * CHUNKS + 4, scratch=rows)(
        *middles, *partners, gain_t, temporal_query, temporal_key, temporal_value)
    keys, values = [], []
    for c in range(CHUNKS):
        forwarded = across(fars[c], 1)
        for value, label in ((fars[c], f"far{c}"), (forwarded, f"way{c}")):
            if label != f"way{CHUNKS - 1}":
                fk, fv = call(far_body, [(part, D)] * 2, 2 * part * D * D * 2, 3 * MIB, n_in=4)(
                    value, gain_t, temporal_key, temporal_value)
                keys.append(fk)
                values.append(fv)
    (refined,) = call(
        views_body, [(own, D)], 10**9, 8 * MIB, n_in=CHUNKS + 4 + 4 * CHUNKS - 2 + 5,
        scratch=[pltpu.VMEM((part, D), BF), pltpu.VMEM((part, D), BF), pltpu.VMEM((own, D), BF)],
    )(*middles, *state, *keys, *values, forwarded, gain_t, temporal_key, temporal_value, temporal_output)
    return refined.reshape(view_maps.shape)


def solution(mesh):
    return jax.shard_map(
        body,
        mesh=mesh,
        in_specs=(P("view", "row", "col", None), P(), P(), P(), P(), P(), P(), P(), P(), P(), P()),
        out_specs=P("view", "row", "col", None),
        check_vma=False,
    )
```

```python
import functools

import jax
import jax.numpy as jnp
from jax import lax
from jax.experimental import pallas as pl
from jax.experimental.pallas import tpu as pltpu
from jax.sharding import PartitionSpec as P


HEADS = 12
HEAD_DIM = 64
RADIUS = 3
CHUNKS = 2
D = 768
GROUP = 4
LANES = GROUP * HEAD_DIM
GROUPS = HEADS // GROUP
ROWS = 4
COLS = 16
TOKENS = ROWS * COLS
SLAB = RADIUS * COLS
SIDE = 32
EDGE = ROWS * RADIUS
CORNER = 2 * RADIUS * RADIUS
KEYS = TOKENS + 2 * SLAB + 2 * SIDE
VIEWS = 4
PART = VIEWS // CHUNKS
ALL_VIEWS = 16
MAP_H = 32
MAP_W = 128

epsilon = 1e-06
very_negative = -1e30
BF = jnp.bfloat16
F32 = jnp.float32
MIB = 1 << 20


def call(body, outs, flops, nbytes, scratch=(), n_in=0, limit=20):
    vmem = pl.BlockSpec(memory_space=pltpu.VMEM)
    return pl.pallas_call(
        body,
        out_shape=tuple(jax.ShapeDtypeStruct(s, BF) if isinstance(s, tuple) else s for s in outs),
        in_specs=[vmem] * n_in,
        out_specs=tuple(vmem for _ in outs),
        scratch_shapes=list(scratch),
        compiler_params=pltpu.CompilerParams(vmem_limit_bytes=limit * MIB),
        cost_estimate=pl.CostEstimate(flops=flops, bytes_accessed=nbytes, transcendentals=0),
    )


def rows_body(maps, a, b, sems):
    odd = lax.axis_index("row") & 1
    copies = [
        pltpu.make_async_copy(maps.at[:, pl.ds(1 - odd, RADIUS)], a, sems.at[0]),
        pltpu.make_async_copy(maps.at[:, pl.ds(odd, RADIUS)], b, sems.at[1]),
    ]
    for copy in copies:
        copy.start()
    for copy in copies:
        copy.wait()


def normed(tokens, gain):
    values = tokens.astype(F32)
    mean = jnp.mean(values * values, axis=-1, keepdims=True)
    return (values * lax.rsqrt(mean + epsilon) * gain[None, :]).astype(BF)


def dot(a, b):
    return jnp.dot(a, b, preferred_element_type=F32)


def own_body(x, gain, wq, q):
    q[...] = (dot(normed(x[...], gain[...]), wq[...]).astype(BF) * 0.125).astype(BF)


def side_base(second):
    odd = lax.axis_index("col") & 1
    return jnp.where(second == (odd == 1), COLS - RADIUS, 0)


def edges_body(x, to_a, to_b):
    shape = (2 * VIEWS * EDGE, VIEWS * TOKENS)
    i = lax.broadcasted_iota(jnp.int32, shape, 0)
    j = lax.broadcasted_iota(jnp.int32, shape, 1)
    second = i >= VIEWS * EDGE
    col = (j & 15) - side_base(second)
    place = EDGE * (j >> 6) + RADIUS * ((j >> 4) & 3) + col + jnp.where(second, VIEWS * EDGE, 0)
    pick = jnp.where((col >= 0) & (col < RADIUS) & (i == place), 1.0, 0.0).astype(BF)
    taken = dot(pick, x[...]).astype(BF)
    to_a[...] = taken[:VIEWS * EDGE]
    to_b[...] = taken[VIEWS * EDGE:]


def corners_body(a, b, to_a, to_b):
    shape = (2 * VIEWS * CORNER, VIEWS * SLAB)
    i = lax.broadcasted_iota(jnp.int32, shape, 0)
    j = lax.broadcasted_iota(jnp.int32, shape, 1)
    second = i >= VIEWS * CORNER
    col = (j & 15) - side_base(second)
    line = j >> 4
    view = (line * 43) >> 7
    place = CORNER * view + RADIUS * (line - RADIUS * view) + col + jnp.where(second, VIEWS * CORNER, 0)
    good = (col >= 0) & (col < RADIUS)
    half = CORNER // 2
    pick_a = jnp.where(good & (i == place), 1.0, 0.0).astype(BF)
    pick_b = jnp.where(good & (i == place + half), 1.0, 0.0).astype(BF)
    taken = (dot(pick_a, a[...]) + dot(pick_b, b[...])).astype(BF)
    to_a[...] = taken[:VIEWS * CORNER]
    to_b[...] = taken[VIEWS * CORNER:]


def slabs_body(x, a, b, gain, wk, wv, k, v, ka, va, kb, vb):
    for source, key, value in ((x, k, v), (a, ka, va), (b, kb, vb)):
        n = normed(source[...], gain[...])
        key[...] = dot(n, wk[...]).astype(BF)
        value[...] = dot(n, wv[...]).astype(BF)


def compact(full, spread):
    full = jnp.where(spread, full, 0.0)
    count = full.shape[0] // GROUP
    result = full[:count]
    for head in range(1, GROUP):
        result = result + full[head * count:(head + 1) * count]
    return result


def attend(q, keys, values, allowed, spread):
    stacked = jnp.concatenate([q] * GROUP, axis=0)
    stacked = jnp.where(spread, stacked, jnp.zeros_like(stacked))
    scores = lax.dot_general(stacked, keys, (((1,), (1,)), ((), ())), preferred_element_type=F32)
    scores = jnp.where(allowed, scores, very_negative)
    highest = jnp.max(scores, axis=-1, keepdims=True)
    weights = jnp.exp(scores - highest)
    share = 1.0 / jnp.sum(weights, axis=-1, keepdims=True)
    return compact(dot(weights.astype(BF), values) * share, spread).astype(BF)


def spread_mask(count):
    shape = (GROUP * count, LANES)
    row = lax.broadcasted_iota(jnp.int32, shape, 0)
    lane = lax.broadcasted_iota(jnp.int32, shape, 1)
    return (row // count) == (lane // HEAD_DIM)


def window_mask(first_row, first_col):
    flat = (1, KEYS)
    j = lax.broadcasted_iota(jnp.int32, flat, 1)
    odd_row = ((first_row >> 2) & 1) == 1
    odd_col = ((first_col >> 4) & 1) == 1
    base_a = jnp.where(odd_row, -RADIUS, ROWS)
    base_b = jnp.where(odd_row, ROWS, -RADIUS)
    slab_a, slab_b, side_a, side_b = TOKENS, TOKENS + SLAB, TOKENS + 2 * SLAB, TOKENS + 2 * SLAB + SIDE
    row = jnp.where(j < slab_a, j >> 4, jnp.where(j < slab_b, ((j - slab_a) >> 4) + base_a, ((j - slab_b) >> 4) + base_b))
    t = (j - side_a) & (SIDE - 1)
    t_row = (t * 43) >> 7
    t_col = t - RADIUS * t_row
    wide_row = jnp.where(t_row < RADIUS, t_row + base_a, jnp.where(t_row < RADIUS + ROWS, t_row - RADIUS, t_row - RADIUS - ROWS + base_b))
    side = j >= side_a
    row = jnp.where(side, wide_row, row)
    at_right = (j >= side_b) == odd_col
    col = jnp.where(side, jnp.where(at_right, t_col + COLS, t_col - RADIUS), j & 15)
    real = jnp.logical_not(side) | (t < RADIUS * (ROWS + 2 * RADIUS))
    there_row, there_col = first_row + row, first_col + col
    inside = (there_row >= 0) & (there_row < MAP_H) & (there_col >= 0) & (there_col < MAP_W)
    row = jnp.where(real & inside, row, 1000)
    shape = (TOKENS, KEYS)
    i = lax.broadcasted_iota(jnp.int32, shape, 0)
    near = (jnp.abs(row - (i >> 4)) <= RADIUS) & (jnp.abs(col - (i & 15)) <= RADIUS)
    tall = jnp.concatenate([near.astype(jnp.int32)] * GROUP, axis=0)
    return tall > 0


def side_tokens(first, edge_a, edge_b, corner_a, corner_b):
    stacked = jnp.concatenate([edge_a[...], edge_b[...], corner_a[...], corner_b[...]], axis=0)
    shape = (PART * 2 * SIDE, 2 * VIEWS * (EDGE + CORNER))
    i = lax.broadcasted_iota(jnp.int32, shape, 0)
    j = lax.broadcasted_iota(jnp.int32, shape, 1)
    view, part, t = (i >> 6) + first, (i >> 5) & 1, i & (SIDE - 1)
    upper, lower = t < RADIUS * RADIUS, t >= RADIUS * (RADIUS + ROWS)
    corner = 2 * VIEWS * EDGE + part * VIEWS * CORNER + view * CORNER + t
    edge = part * VIEWS * EDGE + view * EDGE + t - RADIUS * RADIUS
    source = jnp.where(upper, corner, jnp.where(lower, corner - EDGE, edge))
    pick = jnp.where((j == source) & (t < RADIUS * (ROWS + 2 * RADIUS)), 1.0, 0.0).astype(BF)
    return dot(pick, stacked).astype(BF)


def window_body(chunk, x, q, k, v, ka, va, kb, vb, edge_a, edge_b, corner_a, corner_b, gain, wk, wv, wo, middle, side_k, side_v, out):
    first = chunk * PART
    sides = normed(side_tokens(first, edge_a, edge_b, corner_a, corner_b), gain[...])
    side_k[...] = dot(sides, wk[...]).astype(BF)
    side_v[...] = dot(sides, wv[...]).astype(BF)
    allowed = window_mask(lax.axis_index("row") * ROWS, lax.axis_index("col") * COLS)
    spread = spread_mask(TOKENS)
    for view in range(PART):
        o = slice(view * TOKENS, (view + 1) * TOKENS)
        t = slice((first + view) * TOKENS, (first + view + 1) * TOKENS)
        s = slice((first + view) * SLAB, (first + view + 1) * SLAB)
        e = slice(view * 2 * SIDE, (view + 1) * 2 * SIDE)
        for group in range(GROUPS):
            f = slice(group * LANES, (group + 1) * LANES)
            keys = jnp.concatenate([k[t, f], ka[s, f], kb[s, f], side_k[e, f]], axis=0)
            values = jnp.concatenate([v[t, f], va[s, f], vb[s, f], side_v[e, f]], axis=0)
            out[o, f] = attend(q[t, f], keys, values, allowed, spread)
    middle[...] = (x[first * TOKENS:(first + PART) * TOKENS].astype(F32) + dot(out[...], wo[...])).astype(BF)


def same_place(count):
    shape = (GROUP * TOKENS, count)
    i = lax.broadcasted_iota(jnp.int32, shape, 0)
    j = lax.broadcasted_iota(jnp.int32, shape, 1)
    return (i & 15) == (j & 15)


def row_of(refs, row, f):
    return jnp.concatenate(
        [ref[w * TOKENS + row * COLS:w * TOKENS + (row + 1) * COLS, f] for ref in refs for w in range(ref.shape[0] // TOKENS)],
        axis=0,
    )


def near_body(*refs):
    middles = refs[:CHUNKS]
    gain, wq, wk, wv, q, k, v = refs[CHUNKS:]
    n = normed(jnp.concatenate([r[...] for r in middles], axis=0), gain[...])
    q[...] = (dot(n, wq[...]).astype(BF) * 0.125).astype(BF)
    k[...] = dot(n, wk[...]).astype(BF)
    v[...] = dot(n, wv[...]).astype(BF)


def pair_body(*refs):
    partners = refs[:CHUNKS]
    gain, wk, wv, kp, vp = refs[CHUNKS:]
    n = normed(jnp.concatenate([r[...] for r in partners], axis=0), gain[...])
    kp[...] = dot(n, wk[...]).astype(BF)
    vp[...] = dot(n, wv[...]).astype(BF)


def far_body(far, gain, wk, wv, k, v):
    n = normed(far[...], gain[...])
    k[...] = dot(n, wk[...]).astype(BF)
    v[...] = dot(n, wv[...]).astype(BF)


def views_body(*refs):
    middles, q = refs[:CHUNKS], refs[CHUNKS]
    refs = refs[CHUNKS + 1:]
    count = 2 * CHUNKS + 1
    keys, values = list(refs[:count]), list(refs[count:2 * count])
    last, gain, wk, wv, wo, refined, kl, vl, out = refs[2 * count:]
    far_body(last, gain, wk, wv, kl, vl)
    keys.append(kl)
    values.append(vl)
    spread = spread_mask(TOKENS)
    allowed = same_place(ALL_VIEWS * COLS)
    for row in range(ROWS):
        for group in range(GROUPS):
            f = slice(group * LANES, (group + 1) * LANES)
            full = attend(row_of([q], row, f), row_of(keys, row, f), row_of(values, row, f), allowed, spread)
            for w in range(VIEWS):
                out[w * TOKENS + row * COLS:w * TOKENS + (row + 1) * COLS, f] = full[w * COLS:(w + 1) * COLS]
    middle = jnp.concatenate([r[...] for r in middles], axis=0)
    refined[...] = (middle.astype(F32) + dot(out[...], wo[...])).astype(BF)


def swap(value, axis, first):
    count = lax.axis_size(axis)
    pairs = [(i, i + 1) for i in range(first, count - 1, 2)]
    return lax.ppermute(value, axis, pairs + [(j, i) for i, j in pairs])


def across(value, step):
    return lax.ppermute(value, "view", [(i, i ^ step) for i in range(4)])


def body(
    view_maps,
    gain_spatial,
    spatial_query,
    spatial_key,
    spatial_value,
    spatial_output,
    gain_temporal,
    temporal_query,
    temporal_key,
    temporal_value,
    temporal_output,
):
    own = VIEWS * TOKENS
    part = PART * TOKENS
    x = view_maps.reshape(own, D)
    a, b = call(
        rows_body, [(VIEWS, RADIUS, COLS, D)] * 2, 0, 40 * MIB, n_in=1,
        scratch=[pltpu.SemaphoreType.DMA((2,))],
    )(view_maps)
    slab = VIEWS * SLAB
    a = swap(a, "row", 0).reshape(slab, D)
    b = swap(b, "row", 1).reshape(slab, D)
    edge_a, edge_b = call(edges_body, [(VIEWS * EDGE, D)] * 2, 10**8, MIB, n_in=1)(x)
    edge_a, edge_b = swap(edge_a, "col", 0), swap(edge_b, "col", 1)
    (q,) = call(own_body, [(own, D)], 2 * own * D * D, 2 * MIB, n_in=3)(x, gain_spatial, spatial_query)
    corner_a, corner_b = call(corners_body, [(VIEWS * CORNER, D)] * 2, 10**8, MIB, n_in=2)(a, b)
    corner_a, corner_b = swap(corner_a, "col", 0), swap(corner_b, "col", 1)
    kv = call(
        slabs_body, [(own, D)] * 2 + [(slab, D)] * 4, 2 * (own + 2 * slab) * D * D * 2, 6 * MIB, n_in=6,
    )(x, a, b, gain_spatial, spatial_key, spatial_value)
    middles, fars, partners = [], [], []
    for c in range(CHUNKS):
        (middle,) = call(
            functools.partial(window_body, c), [(part, D)], 10**9, 8 * MIB, n_in=16,
            scratch=[pltpu.VMEM((2 * PART * SIDE, D), BF), pltpu.VMEM((2 * PART * SIDE, D), BF), pltpu.VMEM((part, D), BF)],
        )(x, q, *kv, edge_a, edge_b, corner_a, corner_b, gain_spatial, spatial_key, spatial_value, spatial_output)
        middles.append(middle)
        fars.append(across(middle, 2))
        partners.append(across(middle, 1))
    q, k, v = call(near_body, [(own, D)] * 3, 2 * own * D * D * 3, 6 * MIB, n_in=CHUNKS + 4)(
        *middles, gain_temporal, temporal_query, temporal_key, temporal_value)
    kp, vp = call(pair_body, [(own, D)] * 2, 2 * own * D * D * 2, 6 * MIB, n_in=CHUNKS + 3)(
        *partners, gain_temporal, temporal_key, temporal_value)
    keys, values = [k, kp], [v, vp]
    for c in range(CHUNKS):
        forwarded = across(fars[c], 1)
        for value, label in ((fars[c], f"far{c}"), (forwarded, f"way{c}")):
            if label != f"way{CHUNKS - 1}":
                fk, fv = call(far_body, [(part, D)] * 2, 2 * part * D * D * 2, 3 * MIB, n_in=4)(
                    value, gain_temporal, temporal_key, temporal_value)
                keys.append(fk)
                values.append(fv)
    (refined,) = call(
        views_body, [(own, D)], 10**9, 8 * MIB, n_in=CHUNKS + 1 + 2 * (2 * CHUNKS + 1) + 5,
        scratch=[pltpu.VMEM((part, D), BF), pltpu.VMEM((part, D), BF), pltpu.VMEM((own, D), BF)],
    )(*middles, q, *keys, *values, forwarded, gain_temporal, temporal_key, temporal_value, temporal_output)
    return refined.reshape(view_maps.shape)


def solution(mesh):
    return jax.shard_map(
        body,
        mesh=mesh,
        in_specs=(P("view", "row", "col", None), P(), P(), P(), P(), P(), P(), P(), P(), P(), P()),
        out_specs=P("view", "row", "col", None),
        check_vma=False,
    )
```

```python
import functools

import jax
import jax.numpy as jnp
from jax import lax
from jax.experimental import pallas as pl
from jax.experimental.pallas import tpu as pltpu
from jax.sharding import PartitionSpec as P


HEADS = 12
HEAD_DIM = 64
RADIUS = 3
CHUNKS = 2
D = 768
GROUP = 4
PAIR = 2
LANES = GROUP * HEAD_DIM
GROUPS = HEADS // GROUP
ROWS = 4
COLS = 16
TOKENS = ROWS * COLS
SLAB = RADIUS * COLS
SIDE = 32
EDGE = ROWS * RADIUS
CORNER = 2 * RADIUS * RADIUS
KEYS = TOKENS + 2 * SLAB + 2 * SIDE
VIEWS = 4
PART = VIEWS // CHUNKS
ALL_VIEWS = 16
MAP_H = 32
MAP_W = 128

epsilon = 1e-06
very_negative = -1e30
BF = jnp.bfloat16
F32 = jnp.float32
MIB = 1 << 20


def call(body, outs, flops, nbytes, scratch=(), n_in=0, limit=20):
    vmem = pl.BlockSpec(memory_space=pltpu.VMEM)
    return pl.pallas_call(
        body,
        out_shape=tuple(jax.ShapeDtypeStruct(s, BF) if isinstance(s, tuple) else s for s in outs),
        in_specs=[vmem] * n_in,
        out_specs=tuple(vmem for _ in outs),
        scratch_shapes=list(scratch),
        compiler_params=pltpu.CompilerParams(vmem_limit_bytes=limit * MIB),
        cost_estimate=pl.CostEstimate(flops=flops, bytes_accessed=nbytes, transcendentals=0),
    )


def rows_body(maps, a, b, sems):
    odd = lax.axis_index("row") & 1
    copies = [
        pltpu.make_async_copy(maps.at[:, pl.ds(1 - odd, RADIUS)], a, sems.at[0]),
        pltpu.make_async_copy(maps.at[:, pl.ds(odd, RADIUS)], b, sems.at[1]),
    ]
    for copy in copies:
        copy.start()
    for copy in copies:
        copy.wait()


def normed(tokens, gain):
    values = tokens.astype(F32)
    mean = jnp.mean(values * values, axis=-1, keepdims=True)
    return (values * lax.rsqrt(mean + epsilon) * gain[None, :]).astype(BF)


def dot(a, b):
    return jnp.dot(a, b, preferred_element_type=F32)


def own_body(x, gain, wq, q):
    q[...] = (dot(normed(x[...], gain[...]), wq[...]).astype(BF) * 0.125).astype(BF)


def side_base(second):
    odd = lax.axis_index("col") & 1
    return jnp.where(second == (odd == 1), COLS - RADIUS, 0)


def edges_body(x, to_a, to_b):
    shape = (2 * VIEWS * EDGE, VIEWS * TOKENS)
    i = lax.broadcasted_iota(jnp.int32, shape, 0)
    j = lax.broadcasted_iota(jnp.int32, shape, 1)
    second = i >= VIEWS * EDGE
    col = (j & 15) - side_base(second)
    place = EDGE * (j >> 6) + RADIUS * ((j >> 4) & 3) + col + jnp.where(second, VIEWS * EDGE, 0)
    pick = jnp.where((col >= 0) & (col < RADIUS) & (i == place), 1.0, 0.0).astype(BF)
    taken = dot(pick, x[...]).astype(BF)
    to_a[...] = taken[:VIEWS * EDGE]
    to_b[...] = taken[VIEWS * EDGE:]


def corners_body(a, b, to_a, to_b):
    shape = (2 * VIEWS * CORNER, VIEWS * SLAB)
    i = lax.broadcasted_iota(jnp.int32, shape, 0)
    j = lax.broadcasted_iota(jnp.int32, shape, 1)
    second = i >= VIEWS * CORNER
    col = (j & 15) - side_base(second)
    line = j >> 4
    view = (line * 43) >> 7
    place = CORNER * view + RADIUS * (line - RADIUS * view) + col + jnp.where(second, VIEWS * CORNER, 0)
    good = (col >= 0) & (col < RADIUS)
    half = CORNER // 2
    pick_a = jnp.where(good & (i == place), 1.0, 0.0).astype(BF)
    pick_b = jnp.where(good & (i == place + half), 1.0, 0.0).astype(BF)
    taken = (dot(pick_a, a[...]) + dot(pick_b, b[...])).astype(BF)
    to_a[...] = taken[:VIEWS * CORNER]
    to_b[...] = taken[VIEWS * CORNER:]


def slabs_body(x, a, b, gain, wk, wv, k, v, ka, va, kb, vb):
    for source, key, value in ((x, k, v), (a, ka, va), (b, kb, vb)):
        n = normed(source[...], gain[...])
        key[...] = dot(n, wk[...]).astype(BF)
        value[...] = dot(n, wv[...]).astype(BF)


def compact(full):
    heads = full.shape[1] // HEAD_DIM
    count = full.shape[0] // heads
    tiles = []
    for tile in range(heads // 2):
        lanes = slice(2 * HEAD_DIM * tile, 2 * HEAD_DIM * (tile + 1))
        low = full[2 * tile * count:(2 * tile + 1) * count, lanes]
        high = full[(2 * tile + 1) * count:(2 * tile + 2) * count, lanes]
        tiles.append(jnp.where(lax.broadcasted_iota(jnp.int32, low.shape, 1) < HEAD_DIM, low, high))
    return tiles[0] if len(tiles) == 1 else jnp.concatenate(tiles, axis=1)


def attend(q, keys, values, allowed, spread):
    stacked = jnp.concatenate([q] * (q.shape[1] // HEAD_DIM), axis=0)
    stacked = jnp.where(spread, stacked, jnp.zeros_like(stacked))
    scores = lax.dot_general(stacked, keys, (((1,), (1,)), ((), ())), preferred_element_type=F32)
    scores = jnp.where(allowed, scores, very_negative)
    highest = jnp.max(scores, axis=-1, keepdims=True)
    weights = jnp.exp(scores - highest)
    share = 1.0 / jnp.sum(weights, axis=-1, keepdims=True)
    return compact(dot(weights.astype(BF), values) * share).astype(BF)


def spread_mask(count, heads):
    shape = (heads * count, heads * HEAD_DIM)
    row = lax.broadcasted_iota(jnp.int32, shape, 0)
    lane = lax.broadcasted_iota(jnp.int32, shape, 1)
    return (row // count) == (lane // HEAD_DIM)


def window_mask(first_row, first_col):
    flat = (1, KEYS)
    j = lax.broadcasted_iota(jnp.int32, flat, 1)
    odd_row = ((first_row >> 2) & 1) == 1
    odd_col = ((first_col >> 4) & 1) == 1
    base_a = jnp.where(odd_row, -RADIUS, ROWS)
    base_b = jnp.where(odd_row, ROWS, -RADIUS)
    slab_a, slab_b, side_a, side_b = TOKENS, TOKENS + SLAB, TOKENS + 2 * SLAB, TOKENS + 2 * SLAB + SIDE
    row = jnp.where(j < slab_a, j >> 4, jnp.where(j < slab_b, ((j - slab_a) >> 4) + base_a, ((j - slab_b) >> 4) + base_b))
    t = (j - side_a) & (SIDE - 1)
    t_row = (t * 43) >> 7
    t_col = t - RADIUS * t_row
    wide_row = jnp.where(t_row < RADIUS, t_row + base_a, jnp.where(t_row < RADIUS + ROWS, t_row - RADIUS, t_row - RADIUS - ROWS + base_b))
    side = j >= side_a
    row = jnp.where(side, wide_row, row)
    at_right = (j >= side_b) == odd_col
    col = jnp.where(side, jnp.where(at_right, t_col + COLS, t_col - RADIUS), j & 15)
    real = jnp.logical_not(side) | (t < RADIUS * (ROWS + 2 * RADIUS))
    there_row, there_col = first_row + row, first_col + col
    inside = (there_row >= 0) & (there_row < MAP_H) & (there_col >= 0) & (there_col < MAP_W)
    row = jnp.where(real & inside, row, 1000)
    shape = (TOKENS, KEYS)
    i = lax.broadcasted_iota(jnp.int32, shape, 0)
    near = (jnp.abs(row - (i >> 4)) <= RADIUS) & (jnp.abs(col - (i & 15)) <= RADIUS)
    tall = jnp.concatenate([near.astype(jnp.int32)] * GROUP, axis=0)
    return tall > 0


def side_tokens(first, edge_a, edge_b, corner_a, corner_b):
    stacked = jnp.concatenate([edge_a[...], edge_b[...], corner_a[...], corner_b[...]], axis=0)
    shape = (PART * 2 * SIDE, 2 * VIEWS * (EDGE + CORNER))
    i = lax.broadcasted_iota(jnp.int32, shape, 0)
    j = lax.broadcasted_iota(jnp.int32, shape, 1)
    view, part, t = (i >> 6) + first, (i >> 5) & 1, i & (SIDE - 1)
    upper, lower = t < RADIUS * RADIUS, t >= RADIUS * (RADIUS + ROWS)
    corner = 2 * VIEWS * EDGE + part * VIEWS * CORNER + view * CORNER + t
    edge = part * VIEWS * EDGE + view * EDGE + t - RADIUS * RADIUS
    source = jnp.where(upper, corner, jnp.where(lower, corner - EDGE, edge))
    pick = jnp.where((j == source) & (t < RADIUS * (ROWS + 2 * RADIUS)), 1.0, 0.0).astype(BF)
    return dot(pick, stacked).astype(BF)


def window_body(chunk, x, q, k, v, ka, va, kb, vb, edge_a, edge_b, corner_a, corner_b, gain, wk, wv, wo, middle, side_k, side_v, out):
    first = chunk * PART
    sides = normed(side_tokens(first, edge_a, edge_b, corner_a, corner_b), gain[...])
    side_k[...] = dot(sides, wk[...]).astype(BF)
    side_v[...] = dot(sides, wv[...]).astype(BF)
    allowed = window_mask(lax.axis_index("row") * ROWS, lax.axis_index("col") * COLS)
    spread = spread_mask(TOKENS, GROUP)
    for view in range(PART):
        o = slice(view * TOKENS, (view + 1) * TOKENS)
        t = slice((first + view) * TOKENS, (first + view + 1) * TOKENS)
        s = slice((first + view) * SLAB, (first + view + 1) * SLAB)
        e = slice(view * 2 * SIDE, (view + 1) * 2 * SIDE)
        for group in range(GROUPS):
            f = slice(group * LANES, (group + 1) * LANES)
            keys = jnp.concatenate([k[t, f], ka[s, f], kb[s, f], side_k[e, f]], axis=0)
            values = jnp.concatenate([v[t, f], va[s, f], vb[s, f], side_v[e, f]], axis=0)
            out[o, f] = attend(q[t, f], keys, values, allowed, spread)
    middle[...] = (x[first * TOKENS:(first + PART) * TOKENS].astype(F32) + dot(out[...], wo[...])).astype(BF)


def same_place(count, heads):
    shape = (heads * TOKENS, count)
    i = lax.broadcasted_iota(jnp.int32, shape, 0)
    j = lax.broadcasted_iota(jnp.int32, shape, 1)
    return (i & 15) == (j & 15)


def row_of(refs, row, f):
    return jnp.concatenate(
        [ref[w * TOKENS + row * COLS:w * TOKENS + (row + 1) * COLS, f] for ref in refs for w in range(ref.shape[0] // TOKENS)],
        axis=0,
    )


def near_body(*refs):
    middles = refs[:CHUNKS]
    gain, wq, wk, wv, q, k, v = refs[CHUNKS:]
    n = normed(jnp.concatenate([r[...] for r in middles], axis=0), gain[...])
    q[...] = (dot(n, wq[...]).astype(BF) * 0.125).astype(BF)
    k[...] = dot(n, wk[...]).astype(BF)
    v[...] = dot(n, wv[...]).astype(BF)


def pair_body(*refs):
    partners = refs[:CHUNKS]
    gain, wk, wv, kp, vp = refs[CHUNKS:]
    n = normed(jnp.concatenate([r[...] for r in partners], axis=0), gain[...])
    kp[...] = dot(n, wk[...]).astype(BF)
    vp[...] = dot(n, wv[...]).astype(BF)


def far_body(far, gain, wk, wv, k, v):
    n = normed(far[...], gain[...])
    k[...] = dot(n, wk[...]).astype(BF)
    v[...] = dot(n, wv[...]).astype(BF)


def views_body(*refs):
    middles, q = refs[:CHUNKS], refs[CHUNKS]
    refs = refs[CHUNKS + 1:]
    count = 2 * CHUNKS + 1
    keys, values = list(refs[:count]), list(refs[count:2 * count])
    last, gain, wk, wv, wo, refined, kl, vl, out = refs[2 * count:]
    far_body(last, gain, wk, wv, kl, vl)
    keys.append(kl)
    values.append(vl)
    spread = spread_mask(TOKENS, PAIR)
    allowed = same_place(ALL_VIEWS * COLS, PAIR)
    for row in range(ROWS):
        for pair in range(HEADS // PAIR):
            f = slice(pair * PAIR * HEAD_DIM, (pair + 1) * PAIR * HEAD_DIM)
            full = attend(row_of([q], row, f), row_of(keys, row, f), row_of(values, row, f), allowed, spread)
            for w in range(VIEWS):
                out[w * TOKENS + row * COLS:w * TOKENS + (row + 1) * COLS, f] = full[w * COLS:(w + 1) * COLS]
    middle = jnp.concatenate([r[...] for r in middles], axis=0)
    refined[...] = (middle.astype(F32) + dot(out[...], wo[...])).astype(BF)


def swap(value, axis, first):
    count = lax.axis_size(axis)
    pairs = [(i, i + 1) for i in range(first, count - 1, 2)]
    return lax.ppermute(value, axis, pairs + [(j, i) for i, j in pairs])


def across(value, step):
    return lax.ppermute(value, "view", [(i, i ^ step) for i in range(4)])


def body(
    view_maps,
    gain_spatial,
    spatial_query,
    spatial_key,
    spatial_value,
    spatial_output,
    gain_temporal,
    temporal_query,
    temporal_key,
    temporal_value,
    temporal_output,
):
    own = VIEWS * TOKENS
    part = PART * TOKENS
    x = view_maps.reshape(own, D)
    a, b = call(
        rows_body, [(VIEWS, RADIUS, COLS, D)] * 2, 0, 40 * MIB, n_in=1,
        scratch=[pltpu.SemaphoreType.DMA((2,))],
    )(view_maps)
    slab = VIEWS * SLAB
    a = swap(a, "row", 0).reshape(slab, D)
    b = swap(b, "row", 1).reshape(slab, D)
    edge_a, edge_b = call(edges_body, [(VIEWS * EDGE, D)] * 2, 10**8, MIB, n_in=1)(x)
    edge_a, edge_b = swap(edge_a, "col", 0), swap(edge_b, "col", 1)
    (q,) = call(own_body, [(own, D)], 2 * own * D * D, 2 * MIB, n_in=3)(x, gain_spatial, spatial_query)
    corner_a, corner_b = call(corners_body, [(VIEWS * CORNER, D)] * 2, 10**8, MIB, n_in=2)(a, b)
    corner_a, corner_b = swap(corner_a, "col", 0), swap(corner_b, "col", 1)
    kv = call(
        slabs_body, [(own, D)] * 2 + [(slab, D)] * 4, 2 * (own + 2 * slab) * D * D * 2, 6 * MIB, n_in=6,
    )(x, a, b, gain_spatial, spatial_key, spatial_value)
    middles, fars, partners = [], [], []
    for c in range(CHUNKS):
        (middle,) = call(
            functools.partial(window_body, c), [(part, D)], 10**9, 8 * MIB, n_in=16,
            scratch=[pltpu.VMEM((2 * PART * SIDE, D), BF), pltpu.VMEM((2 * PART * SIDE, D), BF), pltpu.VMEM((part, D), BF)],
        )(x, q, *kv, edge_a, edge_b, corner_a, corner_b, gain_spatial, spatial_key, spatial_value, spatial_output)
        middles.append(middle)
        fars.append(across(middle, 2))
        partners.append(across(middle, 1))
    q, k, v = call(near_body, [(own, D)] * 3, 2 * own * D * D * 3, 6 * MIB, n_in=CHUNKS + 4)(
        *middles, gain_temporal, temporal_query, temporal_key, temporal_value)
    kp, vp = call(pair_body, [(own, D)] * 2, 2 * own * D * D * 2, 6 * MIB, n_in=CHUNKS + 3)(
        *partners, gain_temporal, temporal_key, temporal_value)
    keys, values = [k, kp], [v, vp]
    for c in range(CHUNKS):
        forwarded = across(fars[c], 1)
        for value, label in ((fars[c], f"far{c}"), (forwarded, f"way{c}")):
            if label != f"way{CHUNKS - 1}":
                fk, fv = call(far_body, [(part, D)] * 2, 2 * part * D * D * 2, 3 * MIB, n_in=4)(
                    value, gain_temporal, temporal_key, temporal_value)
                keys.append(fk)
                values.append(fv)
    (refined,) = call(
        views_body, [(own, D)], 10**9, 8 * MIB, n_in=CHUNKS + 1 + 2 * (2 * CHUNKS + 1) + 5,
        scratch=[pltpu.VMEM((part, D), BF), pltpu.VMEM((part, D), BF), pltpu.VMEM((own, D), BF)],
    )(*middles, q, *keys, *values, forwarded, gain_temporal, temporal_key, temporal_value, temporal_output)
    return refined.reshape(view_maps.shape)


def solution(mesh):
    return jax.shard_map(
        body,
        mesh=mesh,
        in_specs=(P("view", "row", "col", None), P(), P(), P(), P(), P(), P(), P(), P(), P(), P()),
        out_specs=P("view", "row", "col", None),
        check_vma=False,
    )
```
